256 devices in a mesh: row: 8 (over z_lo, y), col: 32 (over x, z_hi, core).
Axes of the slice: x: 4, y: 4, z: 8 (z_hi: 4, z_lo: 2; z = z_hi * 2 + z_lo), core: 2. Of those that a mesh axis runs over, the one named last changes fastest.
Arguments:
- object_field: float32 [2, 2, 3072, 12288], P(None, None, 'row', 'col'), may hold values from -5 to 5
- offsets: int32 [32, 32, 2], P('row', 'col'), may hold values from 0 to 256
- amplitudes: float32 [32, 32, 256, 256], P('row', 'col'), may hold values from 0.3 to 3
- probe: float32 [2, 256, 256], replicated, may hold values from -5 to 5
- phase: float32 [256, 256], replicated, may hold values from -3.140625 to 3.140625
Outputs:
- object_grad: float32 [2, 2, 3072, 12288], P(None, None, 'row', 'col')
- probe_grad: float32 [2, 256, 256], replicated
The draws below stay inside these ranges and needn't reach their ends.
All inputs are finite; a program needn't handle non-finite values.
Results may differ from the reference program's by a relative error of at most 0.0003.
Values sent between devices are 32-bit elements; how exact they have to be, the bound alone decides.
A program may use at most 64 MiB of HBM per device.

```python
import math
import jax
import jax.numpy as jnp
from jax import lax

SLICES = 2
TILE = 384
HALO = 64
PROBE = 256
POS = 4
NX = 3072
NY = 12288
NROWPOS = 32
POSITIONS = 1024
N_COL = 32


def set_ends(values, own_key, least, top_value):
    place = [jax.random.randint(jax.random.fold_in(own_key, axis), (), 0, length) for axis, length in enumerate(values.shape)]
    widest = values.shape.index(max(values.shape))
    next_to = place[:widest] + [(place[widest] + 1) % values.shape[widest]] + place[widest + 1:]
    return values.at[tuple(place)].set(least).at[tuple(next_to)].set(top_value)


def levels(stream_key, shape, pieces, least, top_value):
    def one(dim, parts):
        heights = jax.random.uniform(jax.random.fold_in(jax.random.fold_in(stream_key, 6), dim), (parts,), jnp.float32, least / len(pieces), top_value / len(pieces))
        return jnp.repeat(jnp.exp(heights), shape[dim] // parts).reshape((-1,) + (1,) * (len(shape) - dim - 1))

    gain = one(*pieces[0])
    for cut in pieces[1:]:
        gain = gain * one(*cut)
    return gain


def gaussian(stream_key, extent, scale, bound, split=(), held_as=jnp.bfloat16):
    drawn = scale * jax.random.normal(stream_key, extent, jnp.float32)
    if split:
        drawn = drawn * levels(stream_key, extent, split, -0.22, 0.18)
    return jnp.clip(drawn, -bound, bound).astype(held_as)


def setup_inputs(seed: int = 0) -> dict:
    seeds = jax.random.split(jax.random.key(seed), 6)
    return {
        "object_field": gaussian(seeds[0], (SLICES, 2, NX, NY), 0.7, 5.0, ((2, 8), (3, 32)), jnp.float32),
        "offsets": set_ends(jax.random.randint(seeds[1], (NROWPOS, N_COL, 2), 0, TILE + 2 * HALO - PROBE + 1), jax.random.fold_in(seeds[1], 1), 0, TILE + 2 * HALO - PROBE).astype(jnp.int32),
        "amplitudes": jnp.clip(jnp.exp(math.log(3.0) - 2.3025851 * jax.random.uniform(seeds[2], (NROWPOS, N_COL, PROBE, PROBE), jnp.float32) ** levels(seeds[2], (NROWPOS, N_COL, PROBE, PROBE), ((0, 8), (1, 32)), -0.2, 0.2)), 0.3, 3.0),
        "probe": gaussian(seeds[3], (2, PROBE, PROBE), 0.7, 5.0, (), jnp.float32),
        "phase": jnp.clip(jax.random.uniform(seeds[4], (PROBE, PROBE), jnp.float32, -3.140625, 3.140625), -3.140625, 3.140625),
    }


def reference(object_field, offsets, amplitudes, probe, phase):
    obj = lax.complex(object_field[:, 0], object_field[:, 1])
    padded = jnp.pad(obj, ((0, 0), (HALO, HALO), (HALO, HALO)), mode='wrap')
    probe_c = lax.complex(probe[0], probe[1])
    prop = lax.complex(jnp.cos(phase), jnp.sin(phase))
    flat_off = offsets.reshape(NROWPOS * N_COL, 2)
    flat_amp = amplitudes.reshape(NROWPOS * N_COL, PROBE, PROBE)
    accum = jnp.zeros(padded.shape, padded.dtype)
    probe_acc = jnp.zeros(probe_c.shape, probe_c.dtype)

    def fwd(x):
        return jnp.fft.fft2(x, norm='ortho')

    def inv(x):
        return jnp.fft.ifft2(x, norm='ortho')

    def one_step(carry, index):
        accum, probe_acc = carry
        row_dev = index // N_COL // POS
        col_dev = index % N_COL
        start_r = (row_dev * TILE + flat_off[index, 0]).astype(jnp.int32)
        start_c = (col_dev * TILE + flat_off[index, 1]).astype(jnp.int32)
        zero = jnp.zeros((), jnp.int32)
        wins = lax.dynamic_slice(padded, (zero, start_r, start_c), (SLICES, PROBE, PROBE))
        psis = []
        psi = probe_c
        exit_wave = None
        for s in range(SLICES):
            psis.append(psi)
            exit_wave = psi * wins[s]
            if s < SLICES - 1:
                psi = inv(prop * fwd(exit_wave))
        far = fwd(exit_wave)
        magnitude = jnp.sqrt(jnp.real(far) ** 2 + jnp.imag(far) ** 2)
        chi = far - flat_amp[index] * far / jnp.maximum(magnitude, 0.5)
        back = inv(chi)
        grads = [None] * SLICES
        for s in range(SLICES - 1, -1, -1):
            grads[s] = jnp.conj(psis[s]) * back
            if s > 0:
                back = inv(jnp.conj(prop) * fwd(jnp.conj(wins[s]) * back))
            else:
                probe_acc = probe_acc + jnp.conj(wins[0]) * back
        current = lax.dynamic_slice(accum, (zero, start_r, start_c), (SLICES, PROBE, PROBE))
        accum = lax.dynamic_update_slice(accum, current + jnp.stack(grads), (zero, start_r, start_c))
        return ((accum, probe_acc), None)
    (accum, probe_acc), _ = lax.scan(one_step, (accum, probe_acc), jnp.arange(NROWPOS * N_COL, dtype=jnp.int32))
    accum = accum.at[:, NX:NX + HALO, :].add(accum[:, 0:HALO, :])
    accum = accum.at[:, HALO:2 * HALO, :].add(accum[:, NX + HALO:NX + 2 * HALO, :])
    accum = accum[:, HALO:NX + HALO, :]
    accum = accum.at[:, :, NY:NY + HALO].add(accum[:, :, 0:HALO])
    accum = accum.at[:, :, HALO:2 * HALO].add(accum[:, :, NY + HALO:NY + 2 * HALO])
    accum = accum[:, :, HALO:NY + HALO]
    object_grad = jnp.stack([jnp.real(accum), jnp.imag(accum)], axis=1)
    scale = 1.0 / jnp.sqrt(jnp.asarray(POSITIONS, jnp.real(probe_acc).dtype))
    probe_grad = jnp.stack([jnp.real(probe_acc), jnp.imag(probe_acc)]) * scale
    return (object_grad, probe_grad)
```

```python
import math, functools
import numpy as np
import jax, jax.numpy as jnp
from jax import lax
from jax.experimental import pallas as pl
from jax.experimental.pallas import tpu as pltpu
import ml_dtypes
from jax.sharding import PartitionSpec as P

TILE=384; HALO=64; N=256; H=128; POS=4
F32=jnp.float32; BF=jnp.bfloat16

def tables():
    k=np.arange(H)[:,None].astype(np.int64); n=np.arange(H)[None,:].astype(np.int64)
    out=[]
    for odd in (0,1):
        ang=-2*np.pi*(((2*k+odd)*n)%N)/N
        c=np.cos(ang)/16; s=np.sin(ang)/16
        out.append(np.block([[c,-s],[s,c]]))
    fe,fo=out
    t=np.stack([fe,fo,fe.T,fo.T]).astype(np.float32)
    hi=t.astype(ml_dtypes.bfloat16)
    lo=(t-hi.astype(np.float32)).astype(ml_dtypes.bfloat16)
    perm=np.zeros((N,N),np.float32)
    idx=np.concatenate([np.arange(0,N,2),np.arange(1,N,2)])
    perm[np.arange(N),idx]=1
    pm=np.stack([perm,perm.T]).astype(ml_dtypes.bfloat16)
    return hi,lo,pm

def split(x):
    hi=x.astype(BF); lo=(x-hi.astype(F32)).astype(BF)
    return hi,lo

def mm(a,b):
    return jnp.dot(a,b,preferred_element_type=F32)

def left(th,tl,x):
    xh,xl=split(x)
    return mm(jnp.concatenate([th,th,tl],1), jnp.concatenate([xh,xl,xh],0))
def right(x,th,tl):
    xh,xl=split(x)
    return mm(jnp.concatenate([xh,xl,xh],1), jnp.concatenate([th,th,tl],0))

def fwd(t,re,im):
    hi,lo=t
    a=jnp.concatenate([re[:H]+re[H:],im[:H]+im[H:]],0)
    b=jnp.concatenate([re[:H]-re[H:],im[:H]-im[H:]],0)
    ye=left(hi[0],lo[0],a); yo=left(hi[1],lo[1],b)
    re=jnp.concatenate([ye[:H],yo[:H]],0); im=jnp.concatenate([ye[H:],yo[H:]],0)
    a=jnp.concatenate([re[:,:H]+re[:,H:],im[:,:H]+im[:,H:]],1)
    b=jnp.concatenate([re[:,:H]-re[:,H:],im[:,:H]-im[:,H:]],1)
    ye=right(a,hi[2],lo[2]); yo=right(b,hi[3],lo[3])
    return jnp.concatenate([ye[:,:H],yo[:,:H]],1), jnp.concatenate([ye[:,H:],yo[:,H:]],1)

def inv(t,re,im):
    hi,lo=t
    u=right(jnp.concatenate([re[:,:H],im[:,:H]],1),hi[0],lo[0])
    v=right(jnp.concatenate([re[:,H:],im[:,H:]],1),hi[1],lo[1])
    s=u+v; d=u-v
    re=jnp.concatenate([s[:,:H],d[:,:H]],1); im=jnp.concatenate([s[:,H:],d[:,H:]],1)
    u=left(hi[2],lo[2],jnp.concatenate([re[:H],im[:H]],0))
    v=left(hi[3],lo[3],jnp.concatenate([re[H:],im[H:]],0))
    s=u+v; d=u-v
    return jnp.concatenate([s[:H],d[:H]],0), jnp.concatenate([s[H:],d[H:]],0)

def split3(x):
    h=x.astype(BF); r=x-h.astype(F32); m=r.astype(BF); l=(r-m.astype(F32)).astype(BF)
    return h,m,l
def permute(pm,x):
    h,m,l=split3(x)
    y=mm(pm[0],h)+mm(pm[0],m)+mm(pm[0],l)
    h,m,l=split3(y)
    return mm(h,pm[1])+mm(m,pm[1])+mm(l,pm[1])

def compute_kernel(off_ref, obj_ref, ns_ref, ew_ref, co_ref, amp_ref, probe_ref, phase_ref, hi_ref, lo_ref, pm_ref,
                   gt_ref, gns_ref, gew_ref, gco_ref, pg_ref,
                   ext, gext, hc, hs):
    lane64=lax.broadcasted_iota(jnp.int32,(1,128),1)<64
    for s in range(2):
        for c in range(2):
            ext[s,c,0:TILE,0:TILE]=obj_ref[s,c]
            ext[s,c,TILE:512,0:TILE]=ns_ref[s,c]
            p0=ew_ref[s,0,c]; p1=ew_ref[s,1,c]
            ext[s,c,0:192,TILE:512]=jnp.where(lane64,p0,pltpu.roll(p1,64,1))
            ext[s,c,192:384,TILE:512]=jnp.where(lane64,pltpu.roll(p0,64,1),p1)
            for h in range(2):
                cr=co_ref[s,2*h]; cl=co_ref[s,2*h+1]
                if c==0: blk=jnp.where(lane64,cr,pltpu.roll(cl,64,1))
                else: blk=jnp.where(lane64,pltpu.roll(cr,64,1),cl)
                ext[s,c,TILE+64*h:TILE+64*h+64,TILE:512]=blk
    gext[...]=jnp.zeros_like(gext)
    pg_ref[...]=jnp.zeros_like(pg_ref)
    pm=(pm_ref[0],pm_ref[1])
    ph=permute(pm,phase_ref[...])
    hc[...]=jnp.cos(ph); hs[...]=jnp.sin(ph)
    t=([hi_ref[i] for i in range(4)],[lo_ref[i] for i in range(4)])
    rows=lax.broadcasted_iota(jnp.int32,(N,1),0); cols=lax.broadcasted_iota(jnp.int32,(1,N),1)

    def one(p):
        r=off_ref[p,0]; c=off_ref[p,1]
        ra=(rows>=r-64)&(rows<r+192); ca=(cols>=c-64)&(cols<c+192)
        rm=jnp.broadcast_to(ra,(N,N)); cm=jnp.broadcast_to(ca,(N,N))
        def window(s,k):
            e=ext.at[s,k]
            return jnp.where(rm,jnp.where(cm,e[0:N,0:N],e[0:N,N:512]),jnp.where(cm,e[N:512,0:N],e[N:512,N:512]))
        sr=lax.rem(r+192,N); sc=lax.rem(c+192,N)
        br=lax.rem(N-sr,N); bc=lax.rem(N-sc,N)
        def roll(x,a,b):
            return pltpu.roll(pltpu.roll(x,a,0),b,1)
        def scatter(s,k,g):
            e=gext.at[s,k]
            z=jnp.zeros_like(g)
            gr=jnp.where(rm,g,z); gb=jnp.where(rm,z,g)
            e[0:N,0:N]+=jnp.where(cm,gr,z); e[0:N,N:512]+=jnp.where(cm,z,gr)
            e[N:512,0:N]+=jnp.where(cm,gb,z); e[N:512,N:512]+=jnp.where(cm,z,gb)
        pr=roll(probe_ref[0],sr,sc); pi=roll(probe_ref[1],sr,sc)
        wr=window(0,0); wi=window(0,1)
        fr,fi=fwd(t,pr*wr-pi*wi,pr*wi+pi*wr)
        cc=hc[...]; ss=hs[...]
        qr,qi=inv(t,fr*cc-fi*ss,fr*ss+fi*cc)
        wr=window(1,0); wi=window(1,1)
        fr,fi=fwd(t,qr*wr-qi*wi,qr*wi+qi*wr)
        keep=1.0-permute(pm,amp_ref[p])*lax.rsqrt(jnp.maximum(fr*fr+fi*fi,0.25))
        br_,bi_=inv(t,fr*keep,fi*keep)
        scatter(1,0,qr*br_+qi*bi_); scatter(1,1,qr*bi_-qi*br_)
        fr,fi=fwd(t,wr*br_+wi*bi_,wr*bi_-wi*br_)
        cc=hc[...]; ss=hs[...]
        br_,bi_=inv(t,fr*cc+fi*ss,fi*cc-fr*ss)
        scatter(0,0,pr*br_+pi*bi_); scatter(0,1,pr*bi_-pi*br_)
        wr=window(0,0); wi=window(0,1)
        pg_ref[0]+=roll(wr*br_+wi*bi_,br,bc)
        pg_ref[1]+=roll(wr*bi_-wi*br_,br,bc)

    def pair(i,_):
        one(2*i); one(2*i+1)
        return 0
    lax.fori_loop(0,POS//2,pair,0)
    for s in range(2):
        for c in range(2):
            gt_ref[s,c]=gext[s,c,0:TILE,0:TILE]
            gns_ref[s,c]=gext[s,c,TILE:512,0:TILE]
            gew_ref[s,c]=gext[s,c,0:TILE,TILE:512]
            gco_ref[s,c]=gext[s,c,TILE:512,TILE:512]

def compute(off,obj,ns,ew,co,amp,probe,phase,interpret=False):
    hi,lo,pm=tables()
    V=pl.BlockSpec(memory_space=pltpu.VMEM)
    return pl.pallas_call(compute_kernel,
        out_shape=[jax.ShapeDtypeStruct(s,F32) for s in [(2,2,TILE,TILE),(2,2,128,TILE),(2,2,TILE,128),(2,2,128,128),(2,N,N)]],
        in_specs=[pl.BlockSpec(memory_space=pltpu.SMEM)]+[V]*10, out_specs=[V]*5,
        scratch_shapes=[pltpu.VMEM((2,2,512,512),F32)]*2+[pltpu.VMEM((N,N),F32)]*2,
        compiler_params=pltpu.CompilerParams(vmem_limit_bytes=60<<20),
        interpret=interpret,
    )(off,obj,ns,ew,co,amp,probe,phase,jnp.asarray(hi),jnp.asarray(lo),jnp.asarray(pm))


MESH=pl.DeviceIdType.MESH


def place():
    a=lax.axis_index("row"); b=lax.axis_index("col")
    nr=lax.axis_size("row"); nc=lax.axis_size("col")
    return a,b,nr,nc


def greet(partners):
    bar=pltpu.get_barrier_semaphore()
    for d in partners:
        pl.semaphore_signal(bar,inc=1,device_id=d,device_id_type=MESH)
    pl.semaphore_wait(bar,len(partners))


def around(a,b,nr,nc):
    up=lax.rem(a+nr-1,nr); dn=lax.rem(a+1,nr); lf=lax.rem(b+nc-1,nc); rt=lax.rem(b+1,nc)
    return up,dn,lf,rt


def halo_kernel(obj_ref, ns_ref, ew_ref, co_ref, pe, pc, ssem, rsem):
    a,b,nr,nc=place()
    up,dn,lf,rt=around(a,b,nr,nc)
    low=lax.broadcasted_iota(jnp.int32,(1,128),1)<64
    greet([(up,b),(dn,b),(a,lf),(a,rt),(up,lf),(up,rt),(dn,lf),(dn,rt)])
    copies=[]
    def send(src,dst,dev):
        i=len(copies)
        c=pltpu.make_async_remote_copy(src,dst,ssem.at[i],rsem.at[i],device_id=dev,device_id_type=MESH)
        c.start(); copies.append(c)
    for s in range(2):
        send(obj_ref.at[s,:,0:64,:],ns_ref.at[s,:,0:64,:],(up,b))
        send(obj_ref.at[s,:,TILE-64:TILE,:],ns_ref.at[s,:,64:128,:],(dn,b))
        for c in range(2):
            x=obj_ref[s,c,:,0:128]; y=obj_ref[s,c,:,256:384]
            pe[s,0,c]=jnp.where(low,x[0:192],pltpu.roll(x[192:384],64,1))
            pe[s,1,c]=jnp.where(low,pltpu.roll(y[0:192],64,1),y[192:384])
        for h in range(2):
            r0=(TILE-64)*h
            pc[s,2*h]=jnp.where(low,obj_ref[s,0,r0:r0+64,0:128],pltpu.roll(obj_ref[s,1,r0:r0+64,0:128],64,1))
            pc[s,2*h+1]=jnp.where(low,pltpu.roll(obj_ref[s,0,r0:r0+64,256:384],64,1),obj_ref[s,1,r0:r0+64,256:384])
        send(pe.at[s,0],ew_ref.at[s,0],(a,lf))
        send(pe.at[s,1],ew_ref.at[s,1],(a,rt))
        for h,rr in ((0,up),(1,dn)):
            for l,cc in ((0,lf),(1,rt)):
                send(pc.at[s,2*h+l],co_ref.at[s,2*h+l],(rr,cc))
    for c in copies: c.wait()


def halos(obj):
    V=pl.BlockSpec(memory_space=pltpu.VMEM)
    return pl.pallas_call(halo_kernel,
        out_shape=[jax.ShapeDtypeStruct(s,F32) for s in [(2,2,128,TILE),(2,2,2,192,128),(2,4,64,128)]],
        in_specs=[V],out_specs=[V]*3,
        scratch_shapes=[pltpu.VMEM((2,2,2,192,128),F32),pltpu.VMEM((2,4,64,128),F32),
                        pltpu.SemaphoreType.DMA((16,)),pltpu.SemaphoreType.DMA((16,))],
        compiler_params=pltpu.CompilerParams(collective_id=0,has_side_effects=True,vmem_limit_bytes=30<<20),
    )(obj)


def return_kernel(scale, gt_ref, gns_ref, gew_ref, gco_ref, pg_ref, out_ref, pout_ref,
                  pe, pc, rns, rew, rco, half, w1, q1, w2, q2, w3, q3, ag2, ssem, rsem):
    a,b,nr,nc=place()
    up,dn,lf,rt=around(a,b,nr,nc)
    core=lax.rem(b,2); zh=lax.rem(b//2,4); x=b//8
    mate=b+1-2*core
    rows=[lax.rem(a+k,nr) for k in range(1,8)]
    xs=[lax.rem(x+k,4) for k in range(1,4)]
    zs=[lax.rem(zh+k,4) for k in range(1,4)]
    low=lax.broadcasted_iota(jnp.int32,(1,128),1)<64
    greet([(r,b) for r in rows]+[(a,lf),(a,rt),(up,lf),(up,rt),(dn,lf),(dn,rt)]
          +[(a,xx*8+lax.rem(b,8)) for xx in xs]+[(a,x*8+zz*2+core) for zz in zs])
    count=[0]; pend=[]
    def send(src,dst,dev):
        i=count[0]; count[0]+=1
        c=pltpu.make_async_remote_copy(src,dst,ssem.at[i],rsem.at[i],device_id=dev,device_id_type=MESH)
        c.start(); pend.append(c)
        return c
    s1=send(pg_ref.at[1-core],half,(a,mate))
    ret=[]
    for s in range(2):
        for c in range(2):
            e=gew_ref[s,c]
            pe[s,0,c]=jnp.where(low,e[0:192],pltpu.roll(e[192:384],64,1))
            pe[s,1,c]=jnp.where(low,pltpu.roll(e[0:192],64,1),e[192:384])
        for h in range(2):
            u=gco_ref[s,0,64*h:64*h+64]; v=gco_ref[s,1,64*h:64*h+64]
            pc[s,2*h]=jnp.where(low,u,pltpu.roll(v,64,1))
            pc[s,2*h+1]=jnp.where(low,pltpu.roll(u,64,1),v)
    s1.wait_recv()
    for j in range(8):
        w1[j]=half[32*j:32*j+32]+pg_ref[core,32*j:32*j+32]
    st=[send(w1.at[r],q1.at[7-k],(r,b)) for k,r in enumerate(rows)]
    for s in range(2):
        ret.append(send(gns_ref.at[s,:,0:64,:],rns.at[s,:,0:64,:],(dn,b)))
        ret.append(send(gns_ref.at[s,:,64:128,:],rns.at[s,:,64:128,:],(up,b)))
        ret.append(send(pe.at[s,0],rew.at[s,0],(a,rt)))
        ret.append(send(pe.at[s,1],rew.at[s,1],(a,lf)))
        for h,rr in ((0,dn),(1,up)):
            for l,cc in ((0,rt),(1,lf)):
                ret.append(send(pc.at[s,2*h+l],rco.at[s,2*h+l],(rr,cc)))
    out_ref[...]=gt_ref[...]
    for c in st: c.wait_recv()
    t=w1[a]
    for k in range(1,8): t=t+q1[k]
    for j in range(4): w2[j]=t[8*j:8*j+8]
    st=[send(w2.at[xx],q2.at[3-k],(a,xx*8+lax.rem(b,8))) for k,xx in enumerate(xs)]
    for c in st: c.wait_recv()
    t=w2[x]
    for k in range(1,4): t=t+q2[k]
    w3[...]=t
    st=[send(w3,q3.at[zh],(a,x*8+zz*2+core)) for zz in zs]
    q3[zh]=t
    for c in st: c.wait_recv()
    t=((q3[0]+q3[1])+(q3[2]+q3[3]))*scale
    ag2[x]=t
    st=[send(ag2.at[x],ag2.at[x],(a,xx*8+lax.rem(b,8))) for xx in xs]
    for c in st: c.wait_recv()
    for j in range(4): pout_ref[core,a,8*j:8*j+8]=ag2[j]
    st=[send(pout_ref.at[core,a],pout_ref.at[core,a],(r,b)) for r in rows]
    for c in ret: c.wait_recv()
    for s in range(2):
        for c in range(2):
            o=out_ref.at[s,c]
            o[0:64,:]+=rns[s,c,0:64]
            o[TILE-64:TILE,:]+=rns[s,c,64:128]
            p0=rew[s,0,c]; p1=rew[s,1,c]
            z=jnp.zeros_like(p0)
            o[0:192,0:128]+=jnp.where(low,p0,z)
            o[192:384,0:128]+=jnp.where(low,pltpu.roll(p0,64,1),z)
            o[0:192,256:384]+=jnp.where(low,z,pltpu.roll(p1,64,1))
            o[192:384,256:384]+=jnp.where(low,z,p1)
            for h in range(2):
                r0=(TILE-64)*h; z=jnp.zeros((64,128),F32)
                u=rco[s,2*h]; v=rco[s,2*h+1]
                if c==1: u=pltpu.roll(u,64,1)
                if c==0: v=pltpu.roll(v,64,1)
                o[r0:r0+64,0:128]+=jnp.where(low,u,z)
                o[r0:r0+64,256:384]+=jnp.where(low,z,v)
    for c in st: c.wait_recv()
    last=send(pout_ref.at[core],pout_ref.at[core],(a,mate))
    last.wait_recv()
    for c in pend: c.wait_send()


def returned(scale,gt,gns,gew,gco,pg):
    V=pl.BlockSpec(memory_space=pltpu.VMEM)
    n=41
    M=lambda *s: pltpu.VMEM(s,F32)
    return pl.pallas_call(functools.partial(return_kernel,scale),
        out_shape=[jax.ShapeDtypeStruct((2,2,TILE,TILE),F32),jax.ShapeDtypeStruct((2,8,32,N),F32)],
        in_specs=[V]*5,out_specs=[V]*2,
        scratch_shapes=[M(2,2,2,192,128),M(2,4,64,128),M(2,2,128,TILE),M(2,2,2,192,128),M(2,4,64,128),
            M(N,N),M(8,32,N),M(8,32,N),M(4,8,N),M(4,8,N),M(8,N),M(4,8,N),M(4,8,N),
            pltpu.SemaphoreType.DMA((n,)),pltpu.SemaphoreType.DMA((n,))],
        compiler_params=pltpu.CompilerParams(collective_id=1,has_side_effects=True,vmem_limit_bytes=50<<20),
    )(gt,gns,gew,gco,pg)


def local(object_field, offsets, amplitudes, probe, phase):
    ns,ew,co=halos(object_field)
    gt,gns,gew,gco,pg=compute(offsets.reshape(POS,2),object_field,ns,ew,co,amplitudes.reshape(POS,N,N),probe,phase)
    everyone=POS*lax.axis_size("row")*lax.axis_size("col")
    og,pg=returned(1.0/math.sqrt(everyone),gt,gns,gew,gco,pg)
    return og,pg.reshape(2,N,N)


def solution(mesh):
    in_specs=(P(None,None,"row","col"),P("row","col",None),P("row","col",None,None),P(),P())
    out_specs=(P(None,None,"row","col"),P())
    return jax.shard_map(local,mesh=mesh,in_specs=in_specs,out_specs=out_specs,check_vma=False)
```

```python
import math, functools
import numpy as np
import jax, jax.numpy as jnp
from jax import lax
from jax.experimental import pallas as pl
from jax.experimental.pallas import tpu as pltpu
import ml_dtypes
from jax.sharding import PartitionSpec as P

TILE=384; HALO=64; N=256; H=128; POS=4
F32=jnp.float32; BF=jnp.bfloat16

def tables():
    k=np.arange(H)[:,None].astype(np.int64); n=np.arange(H)[None,:].astype(np.int64)
    out=[]
    for odd in (0,1):
        ang=-2*np.pi*(((2*k+odd)*n)%N)/N
        c=np.cos(ang)/16; s=np.sin(ang)/16
        out.append(np.block([[c,-s],[s,c]]))
    fe,fo=out
    t=np.stack([fe,fo,fe.T,fo.T]).astype(np.float32)
    hi=t.astype(ml_dtypes.bfloat16)
    lo=(t-hi.astype(np.float32)).astype(ml_dtypes.bfloat16)
    perm=np.zeros((N,N),np.float32)
    idx=np.concatenate([np.arange(0,N,2),np.arange(1,N,2)])
    perm[np.arange(N),idx]=1
    pm=np.stack([perm,perm.T]).astype(ml_dtypes.bfloat16)
    return hi,lo,pm

def split(x):
    hi=x.astype(BF); lo=(x-hi.astype(F32)).astype(BF)
    return hi,lo

def mm(a,b):
    return jnp.dot(a,b,preferred_element_type=F32)

def left(th,tl,x):
    xh,xl=split(x)
    return mm(jnp.concatenate([th,th,tl],1), jnp.concatenate([xh,xl,xh],0))
def right(x,th,tl):
    xh,xl=split(x)
    return mm(jnp.concatenate([xh,xl,xh],1), jnp.concatenate([th,th,tl],0))

def fwd(t,re,im):
    hi,lo=t
    a=jnp.concatenate([re[:H]+re[H:],im[:H]+im[H:]],0)
    b=jnp.concatenate([re[:H]-re[H:],im[:H]-im[H:]],0)
    ye=left(hi[0],lo[0],a); yo=left(hi[1],lo[1],b)
    re=jnp.concatenate([ye[:H],yo[:H]],0); im=jnp.concatenate([ye[H:],yo[H:]],0)
    a=jnp.concatenate([re[:,:H]+re[:,H:],im[:,:H]+im[:,H:]],1)
    b=jnp.concatenate([re[:,:H]-re[:,H:],im[:,:H]-im[:,H:]],1)
    ye=right(a,hi[2],lo[2]); yo=right(b,hi[3],lo[3])
    return jnp.concatenate([ye[:,:H],yo[:,:H]],1), jnp.concatenate([ye[:,H:],yo[:,H:]],1)

def inv(t,re,im):
    hi,lo=t
    u=right(jnp.concatenate([re[:,:H],im[:,:H]],1),hi[0],lo[0])
    v=right(jnp.concatenate([re[:,H:],im[:,H:]],1),hi[1],lo[1])
    s=u+v; d=u-v
    re=jnp.concatenate([s[:,:H],d[:,:H]],1); im=jnp.concatenate([s[:,H:],d[:,H:]],1)
    u=left(hi[2],lo[2],jnp.concatenate([re[:H],im[:H]],0))
    v=left(hi[3],lo[3],jnp.concatenate([re[H:],im[H:]],0))
    s=u+v; d=u-v
    return jnp.concatenate([s[:H],d[:H]],0), jnp.concatenate([s[H:],d[H:]],0)

def split3(x):
    h=x.astype(BF); r=x-h.astype(F32); m=r.astype(BF); l=(r-m.astype(F32)).astype(BF)
    return h,m,l
def permute(pm,x):
    h,m,l=split3(x)
    y=mm(pm[0],h)+mm(pm[0],m)+mm(pm[0],l)
    h,m,l=split3(y)
    return mm(h,pm[1])+mm(m,pm[1])+mm(l,pm[1])


MESH=pl.DeviceIdType.MESH


def greet(partners):
    bar=pltpu.get_barrier_semaphore()
    for d in partners:
        pl.semaphore_signal(bar,inc=1,device_id=d,device_id_type=MESH)
    return lambda: pl.semaphore_wait(bar,len(partners))


def fused_kernel(scale, off_ref, obj_ref, amp_ref, probe_ref, phase_ref, hi_ref, lo_ref, pm_ref,
                 out_ref, pout_ref,
                 ext, gext, amp, prb, phs, hi, lo, pm, hc, hs, rpr, wave, pg,
                 ns, ew, co, pe, pc, rns, rew, rco, qe, qc,
                 half, w1, q1, w2, q2, w3, q3, ag2, lsem, ssem, rsem):
    a=lax.axis_index("row"); b=lax.axis_index("col")
    nr=lax.axis_size("row"); nc=lax.axis_size("col")
    up=lax.rem(a+nr-1,nr); dn=lax.rem(a+1,nr); lf=lax.rem(b+nc-1,nc); rt=lax.rem(b+1,nc)
    core=lax.rem(b,2); zh=lax.rem(b//2,4); x=b//8
    mate=b+1-2*core
    rows=[lax.rem(a+k,nr) for k in range(1,8)]
    xs=[lax.rem(x+k,4) for k in range(1,4)]
    zs=[lax.rem(zh+k,4) for k in range(1,4)]
    low=lax.broadcasted_iota(jnp.int32,(1,128),1)<64
    met=greet([(r,b) for r in rows]+[(a,lf),(a,rt),(up,lf),(up,rt),(dn,lf),(dn,rt)]
          +[(a,xx*8+lax.rem(b,8)) for xx in xs]+[(a,x*8+zz*2+core) for zz in zs])
    loads=[]
    def load(src,dst):
        c=pltpu.make_async_copy(src,dst,lsem.at[len(loads)]); c.start(); loads.append(c)
        return c
    tiles=[load(obj_ref.at[s],ext.at[s,:,0:TILE,0:TILE]) for s in range(2)]
    small=[load(phase_ref,phs),load(pm_ref,pm),load(amp_ref,amp),load(probe_ref,prb),load(hi_ref,hi),load(lo_ref,lo)]
    count=[0]; pend=[]
    def send(src,dst,dev):
        i=count[0]; count[0]+=1
        c=pltpu.make_async_remote_copy(src,dst,ssem.at[i],rsem.at[i],device_id=dev,device_id_type=MESH)
        c.start(); pend.append(c)
        return c

    def pack(s):
        for c in range(2):
            e=ext.at[s,c]
            pe[s,0,c]=jnp.where(low,e[0:192,0:128],pltpu.roll(e[192:384,0:128],64,1))
            pe[s,1,c]=jnp.where(low,pltpu.roll(e[0:192,256:384],64,1),e[192:384,256:384])
        for h in range(2):
            r0=(TILE-64)*h
            u=ext.at[s,0]; v=ext.at[s,1]
            pc[s,2*h]=jnp.where(low,u[r0:r0+64,0:128],pltpu.roll(v[r0:r0+64,0:128],64,1))
            pc[s,2*h+1]=jnp.where(low,pltpu.roll(u[r0:r0+64,256:384],64,1),v[r0:r0+64,256:384])
    def give(s):
        out=[send(ext.at[s,:,0:64,0:TILE],ns.at[s,:,0:64,:],(up,b)),
             send(ext.at[s,:,TILE-64:TILE,0:TILE],ns.at[s,:,64:128,:],(dn,b)),
             send(pe.at[s,0],ew.at[s,0],(a,lf)),send(pe.at[s,1],ew.at[s,1],(a,rt))]
        for h,rr in ((0,up),(1,dn)):
            for l,cc in ((0,lf),(1,rt)):
                out.append(send(pc.at[s,2*h+l],co.at[s,2*h+l],(rr,cc)))
        return out
    def take(s):
        for c in range(2):
            e=ext.at[s,c]
            e[TILE:512,0:TILE]=ns[s,c]
            p0=ew[s,0,c]; p1=ew[s,1,c]
            e[0:192,TILE:512]=jnp.where(low,p0,pltpu.roll(p1,64,1))
            e[192:384,TILE:512]=jnp.where(low,pltpu.roll(p0,64,1),p1)
            for h in range(2):
                cr=co[s,2*h]; cl=co[s,2*h+1]
                if c==0: cl=pltpu.roll(cl,64,1)
                else: cr=pltpu.roll(cr,64,1)
                e[TILE+64*h:TILE+64*h+64,TILE:512]=jnp.where(low,cr,cl)
    def gpack(s):
        for c in range(2):
            e=gext.at[s,c]
            qe[s,0,c]=jnp.where(low,e[0:192,TILE:512],pltpu.roll(e[192:384,TILE:512],64,1))
            qe[s,1,c]=jnp.where(low,pltpu.roll(e[0:192,TILE:512],64,1),e[192:384,TILE:512])
        for h in range(2):
            r0=TILE+64*h
            u=gext[s,0,r0:r0+64,TILE:512]; v=gext[s,1,r0:r0+64,TILE:512]
            qc[s,2*h]=jnp.where(low,u,pltpu.roll(v,64,1))
            qc[s,2*h+1]=jnp.where(low,pltpu.roll(u,64,1),v)
    def ggive(s):
        out=[send(gext.at[s,:,TILE:TILE+64,0:TILE],rns.at[s,:,0:64,:],(dn,b)),
             send(gext.at[s,:,TILE+64:512,0:TILE],rns.at[s,:,64:128,:],(up,b)),
             send(qe.at[s,0],rew.at[s,0],(a,rt)),send(qe.at[s,1],rew.at[s,1],(a,lf))]
        for h,rr in ((0,dn),(1,up)):
            for l,cc in ((0,rt),(1,lf)):
                out.append(send(qc.at[s,2*h+l],rco.at[s,2*h+l],(rr,cc)))
        return out
    def gtake(s):
        for c in range(2):
            o=out_ref.at[s,c]
            o[0:64,:]+=rns[s,c,0:64]
            o[TILE-64:TILE,:]+=rns[s,c,64:128]
            p0=rew[s,0,c]; p1=rew[s,1,c]
            z=jnp.zeros_like(p0)
            o[0:192,0:128]+=jnp.where(low,p0,z)
            o[192:384,0:128]+=jnp.where(low,pltpu.roll(p0,64,1),z)
            o[0:192,256:384]+=jnp.where(low,z,pltpu.roll(p1,64,1))
            o[192:384,256:384]+=jnp.where(low,z,p1)
            for h in range(2):
                r0=(TILE-64)*h; z=jnp.zeros((64,128),F32)
                u=rco[s,2*h]; v=rco[s,2*h+1]
                if c==1: u=pltpu.roll(u,64,1)
                if c==0: v=pltpu.roll(v,64,1)
                o[r0:r0+64,0:128]+=jnp.where(low,u,z)
                o[r0:r0+64,256:384]+=jnp.where(low,z,v)

    tiles[0].wait(); pack(0)
    tiles[1].wait(); pack(1)
    met()
    got0=give(0)
    got1=give(1)
    gext[...]=jnp.zeros_like(gext)
    pg[...]=jnp.zeros_like(pg)
    for c in small: c.wait()
    pms=(pm[0],pm[1])
    ph=permute(pms,phs[...])
    hc[...]=jnp.cos(ph); hs[...]=jnp.sin(ph)
    def spot(p):
        r=off_ref[p,0,0]; c=off_ref[p,0,1]
        return r,c,lax.rem(r+192,N),lax.rem(c+192,N)
    def roll(v,i,j):
        return pltpu.roll(pltpu.roll(v,i,0),j,1)
    def ready(p,_):
        r,c,sr,sc=spot(p)
        amp[p]=permute(pms,amp[p])
        rpr[p,0]=roll(prb[0],sr,sc); rpr[p,1]=roll(prb[1],sr,sc)
        return 0
    lax.fori_loop(0,POS,ready,0)
    t=([hi[i] for i in range(4)],[lo[i] for i in range(4)])
    ri=lax.broadcasted_iota(jnp.int32,(N,1),0); ci=lax.broadcasted_iota(jnp.int32,(1,N),1)
    def masks(p):
        r,c,_,_=spot(p)
        return (jnp.broadcast_to((ri>=r-64)&(ri<r+192),(N,N)),jnp.broadcast_to((ci>=c-64)&(ci<c+192),(N,N)))
    def window(m,s,k):
        e=ext.at[s,k]; rm,cm=m
        return jnp.where(rm,jnp.where(cm,e[0:N,0:N],e[0:N,N:512]),jnp.where(cm,e[N:512,0:N],e[N:512,N:512]))
    def scatter(m,s,k,g):
        e=gext.at[s,k]; rm,cm=m
        z=jnp.zeros_like(g)
        gr=jnp.where(rm,g,z); gb=jnp.where(rm,z,g)
        e[0:N,0:N]+=jnp.where(cm,gr,z); e[0:N,N:512]+=jnp.where(cm,z,gr)
        e[N:512,0:N]+=jnp.where(cm,gb,z); e[N:512,N:512]+=jnp.where(cm,z,gb)
    def pairs(one):
        def body(i,_):
            one(2*i); one(2*i+1)
            return 0
        lax.fori_loop(0,POS//2,body,0)

    for c in got0: c.wait_recv()
    take(0)
    def first(p):
        m=masks(p)
        pr=rpr[p,0]; pi=rpr[p,1]
        wr=window(m,0,0); wi=window(m,0,1)
        fr,fi=fwd(t,pr*wr-pi*wi,pr*wi+pi*wr)
        cc=hc[...]; ss=hs[...]
        wave[p,0],wave[p,1]=inv(t,fr*cc-fi*ss,fr*ss+fi*cc)
    pairs(first)

    for c in got1: c.wait_recv()
    take(1)
    def second(p):
        m=masks(p)
        qr=wave[p,0]; qi=wave[p,1]
        wr=window(m,1,0); wi=window(m,1,1)
        fr,fi=fwd(t,qr*wr-qi*wi,qr*wi+qi*wr)
        keep=1.0-amp[p]*lax.rsqrt(jnp.maximum(fr*fr+fi*fi,0.25))
        br,bi=inv(t,fr*keep,fi*keep)
        scatter(m,1,0,qr*br+qi*bi); scatter(m,1,1,qr*bi-qi*br)
        wave[p,0]=wr*br+wi*bi; wave[p,1]=wr*bi-wi*br
    pairs(second)
    gpack(1)
    ret1=ggive(1)

    def third(p):
        m=masks(p)
        r,c,sr,sc=spot(p)
        fr,fi=fwd(t,wave[p,0],wave[p,1])
        cc=hc[...]; ss=hs[...]
        br,bi=inv(t,fr*cc+fi*ss,fi*cc-fr*ss)
        wr=window(m,0,0); wi=window(m,0,1)
        ur=lax.rem(N-sr,N); uc=lax.rem(N-sc,N)
        pg[0]+=roll(wr*br+wi*bi,ur,uc)
        pg[1]+=roll(wr*bi-wi*br,ur,uc)
        pr=rpr[p,0]; pi=rpr[p,1]
        wave[p,0]=pr*br+pi*bi; wave[p,1]=pr*bi-pi*br
    pairs(third)

    s1=send(pg.at[1-core],half,(a,mate))
    def fold(p,_):
        m=masks(p)
        for k in range(2): scatter(m,0,k,wave[p,k])
        return 0
    lax.fori_loop(0,POS,fold,0)
    gpack(0)
    s1.wait_recv()
    for j in range(8):
        w1[j]=half[32*j:32*j+32]+pg[core,32*j:32*j+32]
    st=[send(w1.at[r],q1.at[7-k],(r,b)) for k,r in enumerate(rows)]
    ret0=ggive(0)
    for s in range(2):
        for c in range(2):
            out_ref[s,c]=gext[s,c,0:TILE,0:TILE]
    for c in st: c.wait_recv()
    v=w1[a]
    for k in range(1,8): v=v+q1[k]
    for j in range(4): w2[j]=v[8*j:8*j+8]
    st=[send(w2.at[xx],q2.at[3-k],(a,xx*8+lax.rem(b,8))) for k,xx in enumerate(xs)]
    for c in st: c.wait_recv()
    v=w2[x]
    for k in range(1,4): v=v+q2[k]
    w3[...]=v
    st=[send(w3,q3.at[zh],(a,x*8+zz*2+core)) for zz in zs]
    q3[zh]=v
    for c in st: c.wait_recv()
    v=((q3[0]+q3[1])+(q3[2]+q3[3]))*scale
    ag2[x]=v
    st=[send(ag2.at[x],ag2.at[x],(a,xx*8+lax.rem(b,8))) for xx in xs]
    for c in ret1: c.wait_recv()
    gtake(1)
    for c in st: c.wait_recv()
    for j in range(4): pout_ref[core,a,8*j:8*j+8]=ag2[j]
    st=[send(pout_ref.at[core,a],pout_ref.at[core,a],(r,b)) for r in rows]
    for c in ret0: c.wait_recv()
    gtake(0)
    for c in st: c.wait_recv()
    last=send(pout_ref.at[core],pout_ref.at[core],(a,mate))
    last.wait_recv()
    for c in pend: c.wait_send()


def fused(scale,off,obj,amp,probe,phase):
    h,l,m=tables()
    V=pl.BlockSpec(memory_space=pltpu.VMEM); B=pl.BlockSpec(memory_space=pltpu.HBM)
    M=lambda *s: pltpu.VMEM(s,F32)
    n=57
    return pl.pallas_call(functools.partial(fused_kernel,scale),
        out_shape=[jax.ShapeDtypeStruct((2,2,TILE,TILE),F32),jax.ShapeDtypeStruct((2,8,32,N),F32)],
        in_specs=[pl.BlockSpec(memory_space=pltpu.SMEM)]+[B]*7,out_specs=[V]*2,
        scratch_shapes=[M(2,2,512,512),M(2,2,512,512),M(POS,N,N),M(2,N,N),M(N,N),pltpu.VMEM((4,N,N),BF),pltpu.VMEM((4,N,N),BF),
            pltpu.VMEM((2,N,N),BF),M(N,N),M(N,N),M(POS,2,N,N),M(POS,2,N,N),M(2,N,N),
            M(2,2,128,TILE),M(2,2,2,192,128),M(2,4,64,128),M(2,2,2,192,128),M(2,4,64,128),
            M(2,2,128,TILE),M(2,2,2,192,128),M(2,4,64,128),M(2,2,2,192,128),M(2,4,64,128),
            M(N,N),M(8,32,N),M(8,32,N),M(4,8,N),M(4,8,N),M(8,N),M(4,8,N),M(4,8,N),
            pltpu.SemaphoreType.DMA((8,)),pltpu.SemaphoreType.DMA((n,)),pltpu.SemaphoreType.DMA((n,))],
        compiler_params=pltpu.CompilerParams(collective_id=0,has_side_effects=True,vmem_limit_bytes=48<<20),
    )(off,obj,amp,probe,phase,jnp.asarray(h),jnp.asarray(l),jnp.asarray(m))


def local(object_field, offsets, amplitudes, probe, phase):
    everyone=POS*lax.axis_size("row")*lax.axis_size("col")
    og,pgr=fused(1.0/math.sqrt(everyone),offsets,object_field,amplitudes.reshape(POS,N,N),probe,phase)
    return og,pgr.reshape(2,N,N)


def solution(mesh):
    in_specs=(P(None,None,"row","col"),P("row","col",None),P("row","col",None,None),P(),P())
    out_specs=(P(None,None,"row","col"),P())
    return jax.shard_map(local,mesh=mesh,in_specs=in_specs,out_specs=out_specs,check_vma=False)
```

```python
import math, functools
import jax, jax.numpy as jnp
from jax import lax
from jax.experimental import pallas as pl
from jax.experimental.pallas import tpu as pltpu
from jax.sharding import PartitionSpec as P

TILE=384; HALO=64; N=256; H=128; POS=4
F32=jnp.float32; BF=jnp.bfloat16

def make_tables(hi,lo,pm):
    k=lax.broadcasted_iota(jnp.int32,(H,H),0); n=lax.broadcasted_iota(jnp.int32,(H,H),1)
    def wave(m):
        t=jnp.bitwise_and(m,N-1).astype(F32)*(2.0*math.pi/N)
        return jnp.cos(t)*0.0625,-jnp.sin(t)*0.0625
    def put(i,c,s):
        hi[i],lo[i]=split(jnp.concatenate([jnp.concatenate([c,-s],1),jnp.concatenate([s,c],1)],0))
    c,s=wave(2*k*n)
    put(0,c,s); put(2,c,-s)
    c,s=wave((2*k+1)*n)
    put(1,c,s)
    c,s=wave((2*n+1)*k)
    put(3,c,-s)
    i=lax.broadcasted_iota(jnp.int32,(N,N),0); j=lax.broadcasted_iota(jnp.int32,(N,N),1)
    def ones(u,v):
        at=jnp.where(u<H,2*u,2*u-(N-1))
        return jnp.where(v==at,1.0,0.0).astype(BF)
    pm[0]=ones(i,j); pm[1]=ones(j,i)

def split(x):
    hi=x.astype(BF); lo=(x-hi.astype(F32)).astype(BF)
    return hi,lo

def mm(a,b):
    return jnp.dot(a,b,preferred_element_type=F32)

def left(th,tl,x):
    xh,xl=split(x)
    return mm(jnp.concatenate([th,th,tl],1), jnp.concatenate([xh,xl,xh],0))
def right(x,th,tl):
    xh,xl=split(x)
    return mm(jnp.concatenate([xh,xl,xh],1), jnp.concatenate([th,th,tl],0))

def fwd(t,re,im):
    hi,lo=t
    a=jnp.concatenate([re[:H]+re[H:],im[:H]+im[H:]],0)
    b=jnp.concatenate([re[:H]-re[H:],im[:H]-im[H:]],0)
    ye=left(hi[0],lo[0],a); yo=left(hi[1],lo[1],b)
    re=jnp.concatenate([ye[:H],yo[:H]],0); im=jnp.concatenate([ye[H:],yo[H:]],0)
    a=jnp.concatenate([re[:,:H]+re[:,H:],im[:,:H]+im[:,H:]],1)
    b=jnp.concatenate([re[:,:H]-re[:,H:],im[:,:H]-im[:,H:]],1)
    ye=right(a,hi[2],lo[2]); yo=right(b,hi[3],lo[3])
    return jnp.concatenate([ye[:,:H],yo[:,:H]],1), jnp.concatenate([ye[:,H:],yo[:,H:]],1)

def inv(t,re,im):
    hi,lo=t
    u=right(jnp.concatenate([re[:,:H],im[:,:H]],1),hi[0],lo[0])
    v=right(jnp.concatenate([re[:,H:],im[:,H:]],1),hi[1],lo[1])
    s=u+v; d=u-v
    re=jnp.concatenate([s[:,:H],d[:,:H]],1); im=jnp.concatenate([s[:,H:],d[:,H:]],1)
    u=left(hi[2],lo[2],jnp.concatenate([re[:H],im[:H]],0))
    v=left(hi[3],lo[3],jnp.concatenate([re[H:],im[H:]],0))
    s=u+v; d=u-v
    return jnp.concatenate([s[:H],d[:H]],0), jnp.concatenate([s[H:],d[H:]],0)

def split3(x):
    h=x.astype(BF); r=x-h.astype(F32); m=r.astype(BF); l=(r-m.astype(F32)).astype(BF)
    return h,m,l
def permute(pm,x):
    h,m,l=split3(x)
    y=mm(pm[0],h)+mm(pm[0],m)+mm(pm[0],l)
    h,m,l=split3(y)
    return mm(h,pm[1])+mm(m,pm[1])+mm(l,pm[1])


MESH=pl.DeviceIdType.MESH


def greet(partners):
    bar=pltpu.get_barrier_semaphore()
    for d in partners:
        pl.semaphore_signal(bar,inc=1,device_id=d,device_id_type=MESH)
    return lambda: pl.semaphore_wait(bar,len(partners))


def fused_kernel(scale, offs_ref, obj_ref, amp_ref, probe_ref, phase_ref,
                 out_ref, pout_ref,
                 off_ref, ext, gext, amp, prb, phs, hi, lo, pm, hc, hs, rpr, wave, pg,
                 ns, ew, co, pe, pc, rns, rew, rco, qe, qc,
                 half, w1, q1, w2, q2, w3, q3, ag2, pf, lsem, ssem, rsem):
    a=lax.axis_index("row"); b=lax.axis_index("col")
    nr=lax.axis_size("row"); nc=lax.axis_size("col")
    up=lax.rem(a+nr-1,nr); dn=lax.rem(a+1,nr); lf=lax.rem(b+nc-1,nc); rt=lax.rem(b+1,nc)
    core=lax.rem(b,2); zh=lax.rem(b//2,4); x=b//8
    mate=b+1-2*core
    rows=[lax.rem(a+k,nr) for k in range(1,8)]
    xs=[lax.rem(x+k,4) for k in range(1,4)]
    zs=[lax.rem(zh+k,4) for k in range(1,4)]
    low=lax.broadcasted_iota(jnp.int32,(1,128),1)<64
    met=greet([(r,b) for r in rows]+[(a,lf),(a,rt),(up,lf),(up,rt),(dn,lf),(dn,rt)]
          +[(a,xx*8+lax.rem(b,8)) for xx in xs]+[(a,x*8+zz*2+core) for zz in zs])
    loads=[]
    def load(src,dst):
        c=pltpu.make_async_copy(src,dst,lsem.at[len(loads)]); c.start(); loads.append(c)
        return c
    tiles=[load(obj_ref.at[s],ext.at[s,:,0:TILE,0:TILE]) for s in range(2)]
    small=[load(phase_ref,phs),load(amp_ref,amp),load(probe_ref,prb),load(offs_ref,off_ref)]
    count=[0]; pend=[]
    def send(src,dst,dev):
        i=count[0]; count[0]+=1
        c=pltpu.make_async_remote_copy(src,dst,ssem.at[i],rsem.at[i],device_id=dev,device_id_type=MESH)
        c.start(); pend.append(c)
        return c

    def pack(s):
        for c in range(2):
            e=ext.at[s,c]
            pe[s,0,c]=jnp.where(low,e[0:192,0:128],pltpu.roll(e[192:384,0:128],64,1))
            pe[s,1,c]=jnp.where(low,pltpu.roll(e[0:192,256:384],64,1),e[192:384,256:384])
        for h in range(2):
            r0=(TILE-64)*h
            u=ext.at[s,0]; v=ext.at[s,1]
            pc[s,2*h]=jnp.where(low,u[r0:r0+64,0:128],pltpu.roll(v[r0:r0+64,0:128],64,1))
            pc[s,2*h+1]=jnp.where(low,pltpu.roll(u[r0:r0+64,256:384],64,1),v[r0:r0+64,256:384])
    def give(s):
        out=[send(ext.at[s,:,0:64,0:TILE],ns.at[s,:,0:64,:],(up,b)),
             send(ext.at[s,:,TILE-64:TILE,0:TILE],ns.at[s,:,64:128,:],(dn,b)),
             send(pe.at[s,0],ew.at[s,0],(a,lf)),send(pe.at[s,1],ew.at[s,1],(a,rt))]
        for h,rr in ((0,up),(1,dn)):
            for l,cc in ((0,lf),(1,rt)):
                out.append(send(pc.at[s,2*h+l],co.at[s,2*h+l],(rr,cc)))
        return out
    def take(s):
        for c in range(2):
            e=ext.at[s,c]
            e[TILE:512,0:TILE]=ns[s,c]
            p0=ew[s,0,c]; p1=ew[s,1,c]
            e[0:192,TILE:512]=jnp.where(low,p0,pltpu.roll(p1,64,1))
            e[192:384,TILE:512]=jnp.where(low,pltpu.roll(p0,64,1),p1)
            for h in range(2):
                cr=co[s,2*h]; cl=co[s,2*h+1]
                if c==0: cl=pltpu.roll(cl,64,1)
                else: cr=pltpu.roll(cr,64,1)
                e[TILE+64*h:TILE+64*h+64,TILE:512]=jnp.where(low,cr,cl)
    def gpack(s):
        for c in range(2):
            e=gext.at[s,c]
            qe[s,0,c]=jnp.where(low,e[0:192,TILE:512],pltpu.roll(e[192:384,TILE:512],64,1))
            qe[s,1,c]=jnp.where(low,pltpu.roll(e[0:192,TILE:512],64,1),e[192:384,TILE:512])
        for h in range(2):
            r0=TILE+64*h
            u=gext[s,0,r0:r0+64,TILE:512]; v=gext[s,1,r0:r0+64,TILE:512]
            qc[s,2*h]=jnp.where(low,u,pltpu.roll(v,64,1))
            qc[s,2*h+1]=jnp.where(low,pltpu.roll(u,64,1),v)
    def ggive(s):
        out=[send(gext.at[s,:,TILE:TILE+64,0:TILE],rns.at[s,:,0:64,:],(dn,b)),
             send(gext.at[s,:,TILE+64:512,0:TILE],rns.at[s,:,64:128,:],(up,b)),
             send(qe.at[s,0],rew.at[s,0],(a,rt)),send(qe.at[s,1],rew.at[s,1],(a,lf))]
        for h,rr in ((0,dn),(1,up)):
            for l,cc in ((0,rt),(1,lf)):
                out.append(send(qc.at[s,2*h+l],rco.at[s,2*h+l],(rr,cc)))
        return out
    def gtake(s):
        for c in range(2):
            o=gext.at[s,c]
            o[0:64,0:TILE]+=rns[s,c,0:64]
            o[TILE-64:TILE,0:TILE]+=rns[s,c,64:128]
            p0=rew[s,0,c]; p1=rew[s,1,c]
            z=jnp.zeros_like(p0)
            o[0:192,0:128]+=jnp.where(low,p0,z)
            o[192:384,0:128]+=jnp.where(low,pltpu.roll(p0,64,1),z)
            o[0:192,256:384]+=jnp.where(low,z,pltpu.roll(p1,64,1))
            o[192:384,256:384]+=jnp.where(low,z,p1)
            for h in range(2):
                r0=(TILE-64)*h; z=jnp.zeros((64,128),F32)
                u=rco[s,2*h]; v=rco[s,2*h+1]
                if c==1: u=pltpu.roll(u,64,1)
                if c==0: v=pltpu.roll(v,64,1)
                o[r0:r0+64,0:128]+=jnp.where(low,u,z)
                o[r0:r0+64,256:384]+=jnp.where(low,z,v)

    tiles[0].wait(); pack(0)
    tiles[1].wait(); pack(1)
    met()
    got0=give(0)
    got1=give(1)
    gext[...]=jnp.zeros_like(gext)
    pg[...]=jnp.zeros_like(pg)
    make_tables(hi,lo,pm)
    for c in small: c.wait()
    pms=(pm[0],pm[1])
    ph=permute(pms,phs[...])
    hc[...]=jnp.cos(ph); hs[...]=jnp.sin(ph)
    def spot(p):
        r=off_ref[0,p]; c=off_ref[1,p]
        return r,c,lax.rem(r+192,N),lax.rem(c+192,N)
    def roll(v,i,j):
        return pltpu.roll(pltpu.roll(v,i,0),j,1)
    def ready(p,_):
        r,c,sr,sc=spot(p)
        amp[p]=permute(pms,amp[p])
        rpr[p,0]=roll(prb[0],sr,sc); rpr[p,1]=roll(prb[1],sr,sc)
        return 0
    lax.fori_loop(0,POS,ready,0)
    t=([hi[i] for i in range(4)],[lo[i] for i in range(4)])
    ri=lax.broadcasted_iota(jnp.int32,(N,1),0); ci=lax.broadcasted_iota(jnp.int32,(1,N),1)
    def masks(p):
        r,c,_,_=spot(p)
        return (jnp.broadcast_to((ri>=r-64)&(ri<r+192),(N,N)),jnp.broadcast_to((ci>=c-64)&(ci<c+192),(N,N)))
    def window(m,s,k):
        e=ext.at[s,k]; rm,cm=m
        return jnp.where(rm,jnp.where(cm,e[0:N,0:N],e[0:N,N:512]),jnp.where(cm,e[N:512,0:N],e[N:512,N:512]))
    def scatter(m,s,k,g):
        e=gext.at[s,k]; rm,cm=m
        z=jnp.zeros_like(g)
        gr=jnp.where(rm,g,z); gb=jnp.where(rm,z,g)
        e[0:N,0:N]+=jnp.where(cm,gr,z); e[0:N,N:512]+=jnp.where(cm,z,gr)
        e[N:512,0:N]+=jnp.where(cm,gb,z); e[N:512,N:512]+=jnp.where(cm,z,gb)
    def pairs(one):
        def body(i,_):
            one(2*i); one(2*i+1)
            return 0
        lax.fori_loop(0,POS//2,body,0)

    for c in got0: c.wait_recv()
    take(0)
    def first(p):
        m=masks(p)
        pr=rpr[p,0]; pi=rpr[p,1]
        wr=window(m,0,0); wi=window(m,0,1)
        fr,fi=fwd(t,pr*wr-pi*wi,pr*wi+pi*wr)
        cc=hc[...]; ss=hs[...]
        wave[p,0],wave[p,1]=inv(t,fr*cc-fi*ss,fr*ss+fi*cc)
    pairs(first)

    for c in got1: c.wait_recv()
    take(1)
    def second(p):
        m=masks(p)
        qr=wave[p,0]; qi=wave[p,1]
        wr=window(m,1,0); wi=window(m,1,1)
        fr,fi=fwd(t,qr*wr-qi*wi,qr*wi+qi*wr)
        keep=1.0-amp[p]*lax.rsqrt(jnp.maximum(fr*fr+fi*fi,0.25))
        br,bi=inv(t,fr*keep,fi*keep)
        scatter(m,1,0,qr*br+qi*bi); scatter(m,1,1,qr*bi-qi*br)
        wave[p,0]=wr*br+wi*bi; wave[p,1]=wr*bi-wi*br
    pairs(second)
    gpack(1)
    ret1=ggive(1)

    def third(p):
        m=masks(p)
        r,c,sr,sc=spot(p)
        fr,fi=fwd(t,wave[p,0],wave[p,1])
        cc=hc[...]; ss=hs[...]
        br,bi=inv(t,fr*cc+fi*ss,fi*cc-fr*ss)
        wr=window(m,0,0); wi=window(m,0,1)
        ur=lax.rem(N-sr,N); uc=lax.rem(N-sc,N)
        pg[0]+=roll(wr*br+wi*bi,ur,uc)
        pg[1]+=roll(wr*bi-wi*br,ur,uc)
        pr=rpr[p,0]; pi=rpr[p,1]
        wave[p,0]=pr*br+pi*bi; wave[p,1]=pr*bi-pi*br
    pairs(third)

    s1=[send(pg.at[1-core,pl.ds(pl.multiple_of(32*r,32),32)],half.at[k],(a,mate)) for k,r in enumerate(rows+[a])]
    def fold(p,_):
        m=masks(p)
        for k in range(2): scatter(m,0,k,wave[p,k])
        return 0
    lax.fori_loop(0,POS,fold,0)
    gpack(0)
    st=[]
    for k,r in enumerate(rows+[a]):
        s1[k].wait_recv()
        w1[k]=half[k]+pg[core,pl.ds(pl.multiple_of(32*r,32),32)]
        if k<7: st.append(send(w1.at[k],q1.at[6-k],(r,b)))
    ret0=ggive(0)
    for c in st: c.wait_recv()
    v=w1[7]
    for k in range(7): v=v+q1[k]
    for j in range(4): w2[j]=v[8*j:8*j+8]
    st=[send(w2.at[xx],q2.at[3-k],(a,xx*8+lax.rem(b,8))) for k,xx in enumerate(xs)]
    for c in st: c.wait_recv()
    v=w2[x]
    for k in range(1,4): v=v+q2[k]
    w3[...]=v
    st=[send(w3,q3.at[zh],(a,x*8+zz*2+core)) for zz in zs]
    q3[zh]=v
    for c in st: c.wait_recv()
    v=((q3[0]+q3[1])+(q3[2]+q3[3]))*scale
    ag2[x]=v
    st=[send(ag2.at[x],ag2.at[x],(a,xx*8+lax.rem(b,8))) for xx in xs]
    for c in ret1: c.wait_recv()
    gtake(1)
    outs=[load(gext.at[1,:,0:TILE,0:TILE],out_ref.at[1])]
    for c in st: c.wait_recv()
    for j in range(4): pf[core,a,8*j:8*j+8]=ag2[j]
    st=[send(pf.at[core,a],pf.at[core,a],(r,b)) for r in rows]
    fin=[send(pf.at[core,a],pf.at[core,a],(a,mate))]
    for c in ret0: c.wait_recv()
    gtake(0)
    outs.append(load(gext.at[0,:,0:TILE,0:TILE],out_ref.at[0]))
    for k in range(7):
        st[k].wait_recv()
        r=rows[6-k]
        fin.append(send(pf.at[core,r],pf.at[core,r],(a,mate)))
    outs.append(load(pf.at[core],pout_ref.at[core]))
    for c in fin: c.wait_recv()
    outs.append(load(pf.at[1-core],pout_ref.at[1-core]))
    for c in outs: c.wait()
    for c in pend: c.wait_send()


def fused(scale,off,obj,amp,probe,phase):
    B=pl.BlockSpec(memory_space=pltpu.HBM)
    M=lambda *s: pltpu.VMEM(s,F32)
    n=71
    return pl.pallas_call(functools.partial(fused_kernel,scale),
        out_shape=[jax.ShapeDtypeStruct((2,2,TILE,TILE),F32),jax.ShapeDtypeStruct((2,8,32,N),F32)],
        in_specs=[B]*5,out_specs=[B]*2,
        scratch_shapes=[pltpu.SMEM((2,POS),jnp.int32),M(2,2,512,512),M(2,2,512,512),M(POS,N,N),M(2,N,N),M(N,N),pltpu.VMEM((4,N,N),BF),pltpu.VMEM((4,N,N),BF),
            pltpu.VMEM((2,N,N),BF),M(N,N),M(N,N),M(POS,2,N,N),M(POS,2,N,N),M(2,N,N),
            M(2,2,128,TILE),M(2,2,2,192,128),M(2,4,64,128),M(2,2,2,192,128),M(2,4,64,128),
            M(2,2,128,TILE),M(2,2,2,192,128),M(2,4,64,128),M(2,2,2,192,128),M(2,4,64,128),
            M(8,32,N),M(8,32,N),M(7,32,N),M(4,8,N),M(4,8,N),M(8,N),M(4,8,N),M(4,8,N),M(2,8,32,N),
            pltpu.SemaphoreType.DMA((10,)),pltpu.SemaphoreType.DMA((n,)),pltpu.SemaphoreType.DMA((n,))],
        compiler_params=pltpu.CompilerParams(collective_id=0,has_side_effects=True,vmem_limit_bytes=58<<20),
    )(off,obj,amp,probe,phase)


def move_kernel(x_ref, y_ref, ox_ref, oy_ref, xb, yb, isem, osem):
    parts=[(x_ref.at[i//2,i%2],xb.at[i//2,i%2],ox_ref.at[i//2,i%2]) for i in range(4)]+[(y_ref.at[i],yb.at[i],oy_ref.at[i]) for i in range(2)]
    come=[pltpu.make_async_copy(u,v,isem.at[i]) for i,(u,v,_) in enumerate(parts)]
    go=[pltpu.make_async_copy(v,w,osem.at[i]) for i,(_,v,w) in enumerate(parts)]
    for c in come: c.start()
    for c,g in zip(come,go):
        c.wait(); g.start()
    for g in go: g.wait()


def move(x,y):
    B=pl.BlockSpec(memory_space=pltpu.HBM)
    return pl.pallas_call(move_kernel,
        out_shape=[jax.ShapeDtypeStruct(x.shape,F32),jax.ShapeDtypeStruct(y.shape,F32)],
        in_specs=[B]*2,out_specs=[B]*2,
        scratch_shapes=[pltpu.VMEM(x.shape,F32),pltpu.VMEM(y.shape,F32),pltpu.SemaphoreType.DMA((6,)),pltpu.SemaphoreType.DMA((6,))],
        compiler_params=pltpu.CompilerParams(vmem_limit_bytes=58<<20))(x,y)


def local(object_field, offsets, amplitudes, probe, phase):
    everyone=POS*lax.axis_size("row")*lax.axis_size("col")
    og,pgr=fused(1.0/math.sqrt(everyone),offsets.reshape(POS,2).T,object_field,amplitudes.reshape(POS,N,N),probe,phase)
    return move(og,pgr.reshape(2,N,N))


def solution(mesh):
    in_specs=(P(None,None,"row","col"),P("row","col",None),P("row","col",None,None),P(),P())
    out_specs=(P(None,None,"row","col"),P())
    return jax.shard_map(local,mesh=mesh,in_specs=in_specs,out_specs=out_specs,check_vma=False)
```

```python
import math, functools
import jax, jax.numpy as jnp
from jax import lax
from jax.experimental import pallas as pl
from jax.experimental.pallas import tpu as pltpu
from jax.sharding import PartitionSpec as P

TILE=384; HALO=64; N=256; H=128; POS=4
F32=jnp.float32; BF=jnp.bfloat16

def make_tables(hi,lo,pm):
    k=lax.broadcasted_iota(jnp.int32,(H,H),0); n=lax.broadcasted_iota(jnp.int32,(H,H),1)
    def wave(m):
        t=jnp.bitwise_and(m,N-1).astype(F32)*(2.0*math.pi/N)
        return jnp.cos(t)*0.0625,-jnp.sin(t)*0.0625
    def put(i,c,s):
        hi[i],lo[i]=split(jnp.concatenate([jnp.concatenate([c,-s],1),jnp.concatenate([s,c],1)],0))
    c,s=wave(2*k*n)
    put(0,c,s); put(2,c,-s)
    c,s=wave((2*k+1)*n)
    put(1,c,s)
    c,s=wave((2*n+1)*k)
    put(3,c,-s)
    i=lax.broadcasted_iota(jnp.int32,(N,N),0); j=lax.broadcasted_iota(jnp.int32,(N,N),1)
    def ones(u,v):
        at=jnp.where(u<H,2*u,2*u-(N-1))
        return jnp.where(v==at,1.0,0.0).astype(BF)
    pm[0]=ones(i,j); pm[1]=ones(j,i)

def split(x):
    hi=x.astype(BF); lo=(x-hi.astype(F32)).astype(BF)
    return hi,lo

def mm(a,b):
    return jnp.dot(a,b,preferred_element_type=F32)

def left(th,tl,x):
    xh,xl=split(x)
    return mm(jnp.concatenate([th,th,tl],1), jnp.concatenate([xh,xl,xh],0))
def right(x,th,tl):
    xh,xl=split(x)
    return mm(jnp.concatenate([xh,xl,xh],1), jnp.concatenate([th,th,tl],0))

def fwd(t,re,im):
    hi,lo=t
    a=jnp.concatenate([re[:H]+re[H:],im[:H]+im[H:]],0)
    b=jnp.concatenate([re[:H]-re[H:],im[:H]-im[H:]],0)
    ye=left(hi[0],lo[0],a); yo=left(hi[1],lo[1],b)
    re=jnp.concatenate([ye[:H],yo[:H]],0); im=jnp.concatenate([ye[H:],yo[H:]],0)
    a=jnp.concatenate([re[:,:H]+re[:,H:],im[:,:H]+im[:,H:]],1)
    b=jnp.concatenate([re[:,:H]-re[:,H:],im[:,:H]-im[:,H:]],1)
    ye=right(a,hi[2],lo[2]); yo=right(b,hi[3],lo[3])
    return jnp.concatenate([ye[:,:H],yo[:,:H]],1), jnp.concatenate([ye[:,H:],yo[:,H:]],1)

def inv(t,re,im):
    hi,lo=t
    u=right(jnp.concatenate([re[:,:H],im[:,:H]],1),hi[0],lo[0])
    v=right(jnp.concatenate([re[:,H:],im[:,H:]],1),hi[1],lo[1])
    s=u+v; d=u-v
    re=jnp.concatenate([s[:,:H],d[:,:H]],1); im=jnp.concatenate([s[:,H:],d[:,H:]],1)
    u=left(hi[2],lo[2],jnp.concatenate([re[:H],im[:H]],0))
    v=left(hi[3],lo[3],jnp.concatenate([re[H:],im[H:]],0))
    s=u+v; d=u-v
    return jnp.concatenate([s[:H],d[:H]],0), jnp.concatenate([s[H:],d[H:]],0)

def split3(x):
    h=x.astype(BF); r=x-h.astype(F32); m=r.astype(BF); l=(r-m.astype(F32)).astype(BF)
    return h,m,l
def permute(pm,x):
    h,m,l=split3(x)
    y=mm(pm[0],h)+mm(pm[0],m)+mm(pm[0],l)
    h,m,l=split3(y)
    return mm(h,pm[1])+mm(m,pm[1])+mm(l,pm[1])


MESH=pl.DeviceIdType.MESH


def greet(partners):
    bar=pltpu.get_barrier_semaphore()
    for d in partners:
        pl.semaphore_signal(bar,inc=1,device_id=d,device_id_type=MESH)
    return lambda: pl.semaphore_wait(bar,len(partners))


def fused_kernel(scale, offs_ref, obj_ref, amp_ref, probe_ref, phase_ref,
                 out_ref, pout_ref,
                 off_ref, ext, gext, amp, prb, phs, hi, lo, pm, hc, hs, rpr, wave, pg,
                 ns, ew, co, pe, pc, rns, rew, rco, qe, qc,
                 half, w1, q1, w2, q2, w3, q3, ag2, pf, lsem, ssem, rsem):
    a=lax.axis_index("row"); b=lax.axis_index("col")
    nr=lax.axis_size("row"); nc=lax.axis_size("col")
    up=lax.rem(a+nr-1,nr); dn=lax.rem(a+1,nr); lf=lax.rem(b+nc-1,nc); rt=lax.rem(b+1,nc)
    core=lax.rem(b,2); zh=lax.rem(b//2,4); x=b//8
    mate=b+1-2*core
    rows=[lax.rem(a+k,nr) for k in range(1,8)]
    xs=[lax.rem(x+k,4) for k in range(1,4)]
    zs=[lax.rem(zh+k,4) for k in range(1,4)]
    low=lax.broadcasted_iota(jnp.int32,(1,128),1)<64
    met=greet([(r,b) for r in rows]+[(a,lf),(a,rt),(up,lf),(up,rt),(dn,lf),(dn,rt)]
          +[(a,xx*8+lax.rem(b,8)) for xx in xs]+[(a,x*8+zz*2+core) for zz in zs])
    loads=[]
    def load(src,dst):
        c=pltpu.make_async_copy(src,dst,lsem.at[len(loads)]); c.start(); loads.append(c)
        return c
    tiles=[load(obj_ref.at[s],ext.at[s,:,0:TILE,0:TILE]) for s in range(2)]
    small=[load(phase_ref,phs),load(amp_ref,amp),load(probe_ref,prb),load(offs_ref,off_ref)]
    count=[0]; pend=[]
    def send(src,dst,dev):
        i=count[0]; count[0]+=1
        c=pltpu.make_async_remote_copy(src,dst,ssem.at[i],rsem.at[i],device_id=dev,device_id_type=MESH)
        c.start(); pend.append(c)
        return c

    def pack(s):
        for c in range(2):
            e=ext.at[s,c]
            pe[s,0,c]=jnp.where(low,e[0:192,0:128],pltpu.roll(e[192:384,0:128],64,1))
            pe[s,1,c]=jnp.where(low,pltpu.roll(e[0:192,256:384],64,1),e[192:384,256:384])
        for h in range(2):
            r0=(TILE-64)*h
            u=ext.at[s,0]; v=ext.at[s,1]
            pc[s,2*h]=jnp.where(low,u[r0:r0+64,0:128],pltpu.roll(v[r0:r0+64,0:128],64,1))
            pc[s,2*h+1]=jnp.where(low,pltpu.roll(u[r0:r0+64,256:384],64,1),v[r0:r0+64,256:384])
    def give(s):
        out=[send(ext.at[s,:,0:64,0:TILE],ns.at[s,:,0:64,:],(up,b)),
             send(ext.at[s,:,TILE-64:TILE,0:TILE],ns.at[s,:,64:128,:],(dn,b)),
             send(pe.at[s,0],ew.at[s,0],(a,lf)),send(pe.at[s,1],ew.at[s,1],(a,rt))]
        for h,rr in ((0,up),(1,dn)):
            for l,cc in ((0,lf),(1,rt)):
                out.append(send(pc.at[s,2*h+l],co.at[s,2*h+l],(rr,cc)))
        return out
    def take(s):
        for c in range(2):
            e=ext.at[s,c]
            e[TILE:512,0:TILE]=ns[s,c]
            p0=ew[s,0,c]; p1=ew[s,1,c]
            e[0:192,TILE:512]=jnp.where(low,p0,pltpu.roll(p1,64,1))
            e[192:384,TILE:512]=jnp.where(low,pltpu.roll(p0,64,1),p1)
            for h in range(2):
                cr=co[s,2*h]; cl=co[s,2*h+1]
                if c==0: cl=pltpu.roll(cl,64,1)
                else: cr=pltpu.roll(cr,64,1)
                e[TILE+64*h:TILE+64*h+64,TILE:512]=jnp.where(low,cr,cl)
    def gpack(s):
        for c in range(2):
            e=gext.at[s,c]
            qe[s,0,c]=jnp.where(low,e[0:192,TILE:512],pltpu.roll(e[192:384,TILE:512],64,1))
            qe[s,1,c]=jnp.where(low,pltpu.roll(e[0:192,TILE:512],64,1),e[192:384,TILE:512])
        for h in range(2):
            r0=TILE+64*h
            u=gext[s,0,r0:r0+64,TILE:512]; v=gext[s,1,r0:r0+64,TILE:512]
            qc[s,2*h]=jnp.where(low,u,pltpu.roll(v,64,1))
            qc[s,2*h+1]=jnp.where(low,pltpu.roll(u,64,1),v)
    def ggive(s):
        out=[send(gext.at[s,:,TILE:TILE+64,0:TILE],rns.at[s,:,0:64,:],(dn,b)),
             send(gext.at[s,:,TILE+64:512,0:TILE],rns.at[s,:,64:128,:],(up,b)),
             send(qe.at[s,0],rew.at[s,0],(a,rt)),send(qe.at[s,1],rew.at[s,1],(a,lf))]
        for h,rr in ((0,dn),(1,up)):
            for l,cc in ((0,rt),(1,lf)):
                out.append(send(qc.at[s,2*h+l],rco.at[s,2*h+l],(rr,cc)))
        return out
    def gtake(s):
        for c in range(2):
            o=gext.at[s,c]
            o[0:64,0:TILE]+=rns[s,c,0:64]
            o[TILE-64:TILE,0:TILE]+=rns[s,c,64:128]
            p0=rew[s,0,c]; p1=rew[s,1,c]
            z=jnp.zeros_like(p0)
            o[0:192,0:128]+=jnp.where(low,p0,z)
            o[192:384,0:128]+=jnp.where(low,pltpu.roll(p0,64,1),z)
            o[0:192,256:384]+=jnp.where(low,z,pltpu.roll(p1,64,1))
            o[192:384,256:384]+=jnp.where(low,z,p1)
            for h in range(2):
                r0=(TILE-64)*h; z=jnp.zeros((64,128),F32)
                u=rco[s,2*h]; v=rco[s,2*h+1]
                if c==1: u=pltpu.roll(u,64,1)
                if c==0: v=pltpu.roll(v,64,1)
                o[r0:r0+64,0:128]+=jnp.where(low,u,z)
                o[r0:r0+64,256:384]+=jnp.where(low,z,v)

    tiles[0].wait(); pack(0)
    tiles[1].wait(); pack(1)
    met()
    got0=give(0)
    got1=give(1)
    gext[...]=jnp.zeros_like(gext)
    pg[...]=jnp.zeros_like(pg)
    make_tables(hi,lo,pm)
    for c in small: c.wait()
    pms=(pm[0],pm[1])
    ph=permute(pms,phs[...])
    hc[...]=jnp.cos(ph); hs[...]=jnp.sin(ph)
    def spot(p):
        r=off_ref[0,p]; c=off_ref[1,p]
        return r,c,lax.rem(r+192,N),lax.rem(c+192,N)
    def roll(v,i,j):
        return pltpu.roll(pltpu.roll(v,i,0),j,1)
    def ready(p,_):
        r,c,sr,sc=spot(p)
        amp[p]=permute(pms,amp[p])
        rpr[p,0]=roll(prb[0],sr,sc); rpr[p,1]=roll(prb[1],sr,sc)
        return 0
    lax.fori_loop(0,POS,ready,0)
    t=([hi[i] for i in range(4)],[lo[i] for i in range(4)])
    ri=lax.broadcasted_iota(jnp.int32,(N,1),0); ci=lax.broadcasted_iota(jnp.int32,(1,N),1)
    def masks(p):
        r,c,_,_=spot(p)
        return (jnp.broadcast_to((ri>=r-64)&(ri<r+192),(N,N)),jnp.broadcast_to((ci>=c-64)&(ci<c+192),(N,N)))
    def window(m,s,k):
        e=ext.at[s,k]; rm,cm=m
        return jnp.where(rm,jnp.where(cm,e[0:N,0:N],e[0:N,N:512]),jnp.where(cm,e[N:512,0:N],e[N:512,N:512]))
    def scatter(m,s,k,g):
        e=gext.at[s,k]; rm,cm=m
        z=jnp.zeros_like(g)
        gr=jnp.where(rm,g,z); gb=jnp.where(rm,z,g)
        e[0:N,0:N]+=jnp.where(cm,gr,z); e[0:N,N:512]+=jnp.where(cm,z,gr)
        e[N:512,0:N]+=jnp.where(cm,gb,z); e[N:512,N:512]+=jnp.where(cm,z,gb)
    def pairs(one):
        for p in range(POS): one(p)

    for c in got0: c.wait_recv()
    take(0)
    def first(p):
        m=masks(p)
        pr=rpr[p,0]; pi=rpr[p,1]
        wr=window(m,0,0); wi=window(m,0,1)
        fr,fi=fwd(t,pr*wr-pi*wi,pr*wi+pi*wr)
        cc=hc[...]; ss=hs[...]
        wave[p,0],wave[p,1]=inv(t,fr*cc-fi*ss,fr*ss+fi*cc)
    pairs(first)

    for c in got1: c.wait_recv()
    take(1)
    def second(p):
        m=masks(p)
        qr=wave[p,0]; qi=wave[p,1]
        wr=window(m,1,0); wi=window(m,1,1)
        fr,fi=fwd(t,qr*wr-qi*wi,qr*wi+qi*wr)
        keep=1.0-amp[p]*lax.rsqrt(jnp.maximum(fr*fr+fi*fi,0.25))
        br,bi=inv(t,fr*keep,fi*keep)
        scatter(m,1,0,qr*br+qi*bi); scatter(m,1,1,qr*bi-qi*br)
        wave[p,0]=wr*br+wi*bi; wave[p,1]=wr*bi-wi*br
    pairs(second)
    gpack(1)
    ret1=ggive(1)

    def third(p):
        m=masks(p)
        r,c,sr,sc=spot(p)
        fr,fi=fwd(t,wave[p,0],wave[p,1])
        cc=hc[...]; ss=hs[...]
        br,bi=inv(t,fr*cc+fi*ss,fi*cc-fr*ss)
        wr=window(m,0,0); wi=window(m,0,1)
        ur=lax.rem(N-sr,N); uc=lax.rem(N-sc,N)
        pg[0]+=roll(wr*br+wi*bi,ur,uc)
        pg[1]+=roll(wr*bi-wi*br,ur,uc)
        pr=rpr[p,0]; pi=rpr[p,1]
        wave[p,0]=pr*br+pi*bi; wave[p,1]=pr*bi-pi*br
    pairs(third)

    s1=[send(pg.at[1-core,pl.ds(pl.multiple_of(32*r,32),32)],half.at[k],(a,mate)) for k,r in enumerate(rows+[a])]
    def fold(p,_):
        m=masks(p)
        for k in range(2): scatter(m,0,k,wave[p,k])
        return 0
    lax.fori_loop(0,POS,fold,0)
    gpack(0)
    st=[]
    for k,r in enumerate(rows+[a]):
        s1[k].wait_recv()
        w1[k]=half[k]+pg[core,pl.ds(pl.multiple_of(32*r,32),32)]
        if k<7: st.append(send(w1.at[k],q1.at[6-k],(r,b)))
    ret0=ggive(0)
    for c in st: c.wait_recv()
    v=w1[7]
    for k in range(7): v=v+q1[k]
    for j in range(4): w2[j]=v[8*j:8*j+8]
    st=[send(w2.at[xx],q2.at[3-k],(a,xx*8+lax.rem(b,8))) for k,xx in enumerate(xs)]
    for c in st: c.wait_recv()
    v=w2[x]
    for k in range(1,4): v=v+q2[k]
    w3[...]=v
    st=[send(w3,q3.at[zh],(a,x*8+zz*2+core)) for zz in zs]
    q3[zh]=v
    for c in st: c.wait_recv()
    v=((q3[0]+q3[1])+(q3[2]+q3[3]))*scale
    ag2[x]=v
    st=[send(ag2.at[x],ag2.at[x],(a,xx*8+lax.rem(b,8))) for xx in xs]
    for c in ret1: c.wait_recv()
    gtake(1)
    outs=[load(gext.at[1,:,0:TILE,0:TILE],out_ref.at[1])]
    for c in st: c.wait_recv()
    for j in range(4): pf[core,a,8*j:8*j+8]=ag2[j]
    st=[send(pf.at[core,a],pf.at[core,a],(r,b)) for r in rows]
    fin=[send(pf.at[core,a],pf.at[core,a],(a,mate))]
    for c in ret0: c.wait_recv()
    gtake(0)
    outs.append(load(gext.at[0,:,0:TILE,0:TILE],out_ref.at[0]))
    for k in range(7):
        st[k].wait_recv()
        r=rows[6-k]
        fin.append(send(pf.at[core,r],pf.at[core,r],(a,mate)))
    outs.append(load(pf.at[core],pout_ref.at[core]))
    for c in fin: c.wait_recv()
    outs.append(load(pf.at[1-core],pout_ref.at[1-core]))
    for c in outs: c.wait()
    for c in pend: c.wait_send()


def fused(scale,off,obj,amp,probe,phase):
    B=pl.BlockSpec(memory_space=pltpu.HBM)
    M=lambda *s: pltpu.VMEM(s,F32)
    n=71
    return pl.pallas_call(functools.partial(fused_kernel,scale),
        out_shape=[jax.ShapeDtypeStruct((2,2,TILE,TILE),F32),jax.ShapeDtypeStruct((2,8,32,N),F32)],
        in_specs=[B]*5,out_specs=[B]*2,
        scratch_shapes=[pltpu.SMEM((2,POS),jnp.int32),M(2,2,512,512),M(2,2,512,512),M(POS,N,N),M(2,N,N),M(N,N),pltpu.VMEM((4,N,N),BF),pltpu.VMEM((4,N,N),BF),
            pltpu.VMEM((2,N,N),BF),M(N,N),M(N,N),M(POS,2,N,N),M(POS,2,N,N),M(2,N,N),
            M(2,2,128,TILE),M(2,2,2,192,128),M(2,4,64,128),M(2,2,2,192,128),M(2,4,64,128),
            M(2,2,128,TILE),M(2,2,2,192,128),M(2,4,64,128),M(2,2,2,192,128),M(2,4,64,128),
            M(8,32,N),M(8,32,N),M(7,32,N),M(4,8,N),M(4,8,N),M(8,N),M(4,8,N),M(4,8,N),M(2,8,32,N),
            pltpu.SemaphoreType.DMA((10,)),pltpu.SemaphoreType.DMA((n,)),pltpu.SemaphoreType.DMA((n,))],
        compiler_params=pltpu.CompilerParams(collective_id=0,has_side_effects=True,vmem_limit_bytes=58<<20),
    )(off,obj,amp,probe,phase)


def move_kernel(x_ref, y_ref, ox_ref, oy_ref, xb, yb, isem, osem):
    def cut(u,i): return u.at[i//6,i//3%2,i%3*128:i%3*128+128]
    parts=[(cut(x_ref,i),cut(xb,i),cut(ox_ref,i)) for i in range(12)]+[(y_ref.at[i],yb.at[i],oy_ref.at[i]) for i in range(2)]
    come=[pltpu.make_async_copy(u,v,isem.at[i]) for i,(u,v,_) in enumerate(parts)]
    go=[pltpu.make_async_copy(v,w,osem.at[i]) for i,(_,v,w) in enumerate(parts)]
    for c in come: c.start()
    for c,g in zip(come,go):
        c.wait(); g.start()
    for g in go: g.wait()


def move(x,y):
    B=pl.BlockSpec(memory_space=pltpu.HBM)
    return pl.pallas_call(move_kernel,
        out_shape=[jax.ShapeDtypeStruct(x.shape,F32),jax.ShapeDtypeStruct(y.shape,F32)],
        in_specs=[B]*2,out_specs=[B]*2,
        scratch_shapes=[pltpu.VMEM(x.shape,F32),pltpu.VMEM(y.shape,F32),pltpu.SemaphoreType.DMA((14,)),pltpu.SemaphoreType.DMA((14,))],
        compiler_params=pltpu.CompilerParams(vmem_limit_bytes=58<<20))(x,y)


def local(object_field, offsets, amplitudes, probe, phase):
    everyone=POS*lax.axis_size("row")*lax.axis_size("col")
    og,pgr=fused(1.0/math.sqrt(everyone),offsets.reshape(POS,2).T,object_field,amplitudes.reshape(POS,N,N),probe,phase)
    return move(og,pgr.reshape(2,N,N))


def solution(mesh):
    in_specs=(P(None,None,"row","col"),P("row","col",None),P("row","col",None,None),P(),P())
    out_specs=(P(None,None,"row","col"),P())
    return jax.shard_map(local,mesh=mesh,in_specs=in_specs,out_specs=out_specs,check_vma=False)
```
